128 devices in a mesh: rows: 32 (over x, y, core), cols: 4 (over z).
Axes of the slice: x: 4, y: 4, z: 4, core: 2. Of those that a mesh axis runs over, the one named last changes fastest.
Arguments:
- history_owner: int32 [128, 1024, 1], P('rows'), may hold values from 0 to 31; in each aligned block of 1024 rows (0 to 1023, 1024 to 2047, ..., all dimensions but the last counted through in order) at most 48 rows name the same one
- history_row: int32 [128, 1024], P('rows'), may hold values from 0 to 4095
- candidate_owner: int32 [128, 512, 1], P('rows'), may hold values from 0 to 31; in each aligned block of 512 rows (0 to 511, 512 to 1023, ..., all dimensions but the last counted through in order) at most 24 rows name the same one
- candidate_row: int32 [128, 512], P('rows'), may hold values from 0 to 4095
- history_length: int32 [128], P('rows'), may hold values from 256 to 1024, as said below
- embed_table: bfloat16 [131072, 1024], P('rows', 'cols'), may hold values from -7 to 7
- query_weight: bfloat16 [2, 1024, 1024], replicated, may hold values from -9 to 9
- output_weight: bfloat16 [2, 1024, 1024], replicated, may hold values from -0.1875 to 0.1875
- score_weight: float32 [1024], replicated, may hold values from -0.1875 to 0.1875
- logit_grad: float32 [128, 512], P(('rows', 'cols')), may hold values from -192 to 192
Outputs:
- logits: float32 [128, 512], P(('rows', 'cols'))
- table_grad: float32 [131072, 1024], P('rows', 'cols')
The draws below stay inside these ranges and needn't reach their ends.
Inputs may be any that keep to these rules, and one draw needn't show every extreme that they name: `history_owner`: within one user's history no owner index is named more than 48 times. `candidate_owner`: within one user's candidates no owner index is named more than 24 times. `history_length`: some user's length is 1024.
All inputs are finite; a program needn't handle non-finite values.
Results may differ from the reference program's by a relative error of at most 0.033.
The reference program's roundings to bfloat16 on the way (of `history`, `queries`, `weights` and `attended`) count: a program that leaves them out, or rounds other values in their place, can miss the bound.
Values may be sent and summed in bfloat16 or wider, within the bound.
No kernel may reach another device: no remote copies, remote signals or barrier semaphores. Data moves between devices by JAX's collectives and lax.ppermute only.
A program may use at most 192 MiB of HBM per device.

```python
import math
import jax
import jax.numpy as jnp
import numpy as np
from jax import lax

D = 1024
HEADS = 8
LAYERS = 2
HIST = 1024
CAND = 512
TAB_DEV = 4096
USERS = 128
TABLE_ROWS = 131072
MOST_H = 48
MOST_C = 24
N_ROWS = 32


def draw_embed_table(key, part):
    key_vals = jax.random.fold_in(key, 0)
    values = jnp.clip(jax.random.normal(key_vals, (TABLE_ROWS, D), jnp.float32), -6.0, 6.0)
    return values.astype(jnp.bfloat16)


def draw_query_weight(key, part):
    jitter = jnp.clip(jax.random.normal(key, (LAYERS, D, D), jnp.float32), -6.0, 6.0) / math.sqrt(D)
    return jitter.astype(jnp.bfloat16)


def draw_history_length(key, part):
    lengths = jax.random.randint(key, (USERS,), HIST // 4, HIST + 1, dtype=jnp.int32)
    return lengths.at[0].set(HIST)


def place_ends(entries, key, smallest, top_value):
    dims = entries.shape
    place = [jax.random.randint(jax.random.fold_in(key, axis), (), 0, dims[axis]) for axis in range(len(dims))]
    entries = entries.at[tuple(place)].set(smallest)
    longest = dims.index(max(dims))
    place[longest] = (place[longest] + 1) % dims[longest]
    return entries.at[tuple(place)].set(top_value)


def steps_of(own_key, shape, cuts, least, top_value):
    loudness, own = 1.0, jax.random.fold_in(own_key, 6)
    for dim, parts in cuts:
        draws = jnp.exp(jax.random.uniform(jax.random.fold_in(own, dim), (parts,), jnp.float32, least / len(cuts), top_value / len(cuts)))
        loudness = loudness * jnp.repeat(draws, shape[dim] // parts).reshape([-1 if axis == dim else 1 for axis in range(len(shape))])
    return loudness


def assign_block(stream_key, own, number, rows, count, top, bound, slope):
    order = jax.random.permutation(stream_key, count)
    crowded, common = load_shares(count, rows * top, bound, slope, True), load_shares(count, rows * top, bound, slope, False)
    places = jnp.arange(count)

    def named(tallies, offset_by):
        used = int((tallies > 0).sum())
        fixed = max(1, used // 4)
        shifted = fixed + (places - fixed + offset_by * (used - fixed)) % max(1, count - fixed)
        return jnp.zeros((count,), jnp.int32).at[order[jnp.where(places < fixed, places, shifted)]].set(jnp.asarray(tallies, jnp.int32))

    tallies = jnp.where(number % 4 == 0, named(crowded, number // 4), named(common, number - number // 4 - 1))
    mixed = jax.random.permutation(jax.random.fold_in(own, 3), count)
    giver, taker = mixed[0:count // 2 * 2:2], mixed[1:count // 2 * 2:2]
    room = jnp.minimum(tallies[giver] - 1, bound - tallies[taker]) // 2
    room = jnp.where((giver == order[0]) | (taker == order[0]) | (tallies[taker] == 0), 0, jnp.maximum(room, 0))
    shifted = jax.random.randint(jax.random.fold_in(own, 4), (count // 2,), 0, 1 << 20) % (room + 1)
    tallies = tallies.at[giver].add(-shifted).at[taker].add(shifted)
    members = jnp.searchsorted(jnp.cumsum(tallies), jnp.arange(rows * top), side="right").astype(jnp.int32)
    grid = members.reshape(top, rows).T
    grid = grid[jax.random.permutation(jax.random.fold_in(own, 1), rows)]
    offset_by = jax.random.randint(jax.random.fold_in(own, 2), (rows, 1), 0, top)
    return jnp.take_along_axis(grid, (jnp.arange(top)[None, :] + offset_by) % top, axis=1)


def load_shares(number_of, total, reach, slope, full):
    portions = [(1 << 20) // math.isqrt(rank ** slope) + 1 for rank in range(1, number_of + 1)]
    largest = reach if full else min(reach, max(-(-total // number_of), total * portions[0] // sum(portions)))
    least = 1 if total - largest >= number_of - 1 else 0
    given, rest = [largest] + [least] * (number_of - 1), total - largest - least * (number_of - 1)
    while rest > 0:
        movable = [i for i in range(1, number_of) if given[i] < largest] or [i for i in range(1, number_of) if given[i] < reach]
        mass, budget = sum([portions[i] for i in movable]), rest
        for i in movable:
            more = min(reach - given[i], max(1, budget * portions[i] // mass), rest)
            given[i] = given[i] + more
            rest = rest - more
    return np.array(given)


def scatter_about(stream_key, extent, scale, bound, shards=(), kind=jnp.bfloat16):
    gain = steps_of(stream_key, extent, shards, -0.22, 0.18) if shards else 1.0
    array = jax.random.normal(stream_key, extent, jnp.float32) * scale * gain
    return jnp.minimum(jnp.maximum(array, -bound), bound).astype(kind)


def setup_inputs(seed: int = 0) -> dict:
    keys = jax.random.split(jax.random.key(seed), 11)
    history_owner_keys = jax.random.split(jax.random.fold_in(keys[0], 1), USERS * HIST // HIST)
    history_owner_turns = jax.random.permutation(jax.random.fold_in(keys[0], 3), USERS * HIST // HIST)
    history_owner = jax.vmap(lambda own, number: assign_block(jax.random.fold_in(keys[0], 2), own, number, HIST, N_ROWS, 1, MOST_H, 2))(history_owner_keys, history_owner_turns).reshape((USERS, HIST, 1))
    history_row = place_ends(jax.random.randint(keys[1], (USERS, HIST), 0, TAB_DEV), jax.random.fold_in(keys[1], 1), 0, TAB_DEV - 1).astype(jnp.int32)
    candidate_owner_keys = jax.random.split(jax.random.fold_in(keys[2], 1), USERS * CAND // CAND)
    candidate_owner_turns = jax.random.permutation(jax.random.fold_in(keys[2], 3), USERS * CAND // CAND)
    candidate_owner = jax.vmap(lambda own, number: assign_block(jax.random.fold_in(keys[2], 2), own, number, CAND, N_ROWS, 1, MOST_C, 2))(candidate_owner_keys, candidate_owner_turns).reshape((USERS, CAND, 1))
    candidate_row = place_ends(jax.random.randint(keys[3], (USERS, CAND), 0, TAB_DEV), jax.random.fold_in(keys[3], 1), 0, TAB_DEV - 1).astype(jnp.int32)
    history_length = draw_history_length(jax.random.fold_in(keys[10], 71), 0)
    embed_table = draw_embed_table(jax.random.fold_in(keys[10], 71), 0)
    query_weight = draw_query_weight(jax.random.fold_in(keys[10], 71), 0)
    output_weight = scatter_about(keys[7], (LAYERS, D, D), D ** -0.5, 0.1875)
    score_weight = scatter_about(keys[8], (D,), D ** -0.5, 0.1875, (), jnp.float32)
    logit_grad = scatter_about(keys[9], (USERS, CAND), 32.0, 192.0, ((0, 128),), jnp.float32)
    return dict(history_owner=history_owner, history_row=history_row, candidate_owner=candidate_owner, candidate_row=candidate_row, history_length=history_length, embed_table=embed_table, query_weight=query_weight, output_weight=output_weight, score_weight=score_weight, logit_grad=logit_grad)


def user_pass(history, candidate, length, query_weight, output_weight, score_weight):
    hist_len = history.shape[0]
    width = history.shape[1]
    head_dim = width // HEADS
    inv_root = 1.0 / math.sqrt(head_dim)
    key_heads = history.reshape(hist_len, HEADS, head_dim)
    visible = jnp.arange(hist_len) < length
    stream = candidate
    for layer_id in range(query_weight.shape[0]):
        queries = jnp.dot(stream.astype(jnp.bfloat16), query_weight[layer_id], preferred_element_type=jnp.float32).astype(jnp.bfloat16)
        query_heads = queries.astype(jnp.float32).reshape(-1, HEADS, head_dim)
        scores = jnp.einsum('chd,jhd->hcj', query_heads, key_heads) * inv_root
        scores = jnp.where(visible[None, None, :], scores, -jnp.inf)
        weights = jax.nn.softmax(scores, axis=-1).astype(jnp.bfloat16)
        attended = jnp.einsum('hcj,jhd->chd', weights.astype(jnp.float32), key_heads).astype(jnp.bfloat16)
        stream = stream + jnp.dot(attended.reshape(-1, width), output_weight[layer_id], preferred_element_type=jnp.float32)
    return jnp.dot(stream, score_weight, precision=lax.Precision.HIGHEST)

def reference(history_owner, history_row, candidate_owner, candidate_row, history_length, embed_table, query_weight, output_weight, score_weight, logit_grad):
    history_key = (history_owner[:, :, 0] * TAB_DEV + history_row).astype(jnp.int32)
    candidate_key = (candidate_owner[:, :, 0] * TAB_DEV + candidate_row).astype(jnp.int32)

    def advance(summed, packed):
        hist_key, cand_key, length, cotangent = packed
        history = embed_table[hist_key].astype(jnp.float32)
        candidate = embed_table[cand_key].astype(jnp.float32)

        def forward(hist_in, cand_in):
            return user_pass(hist_in, cand_in, length, query_weight, output_weight, score_weight)
        logits, backward = jax.vjp(forward, history, candidate)
        hist_grad, cand_grad = backward(cotangent)
        summed = summed.at[hist_key].add(hist_grad).at[cand_key].add(cand_grad)
        return (summed, logits)
    initial = jnp.zeros(embed_table.shape, jnp.float32)
    table_grad, logits = lax.scan(advance, initial, (history_key, candidate_key, history_length, logit_grad))
    return (logits, table_grad)
```

```python
import functools
import math

import jax
import jax.numpy as jnp
from jax import lax
from jax.experimental import pallas as pl
from jax.experimental.pallas import tpu as pltpu
from jax.sharding import PartitionSpec as P

HEADS = 8
BF = jnp.bfloat16
F32 = jnp.float32
NN = (((1,), (0,)), ((), ()))
NT = (((1,), (1,)), ((), ()))
TN = (((0,), (0,)), ((), ()))
VMEM_SPEC = pl.BlockSpec(memory_space=pltpu.VMEM)
SMEM_SPEC = pl.BlockSpec(memory_space=pltpu.SMEM)
MIB = 1024 * 1024


def dot(a, b, dims):
    return lax.dot_general(a, b, dims, preferred_element_type=F32)


def iota(shape, axis):
    return lax.broadcasted_iota(jnp.int32, shape, axis)


def request_kernel(me, h_own, h_row, c_own, c_row, req, h_pos, c_pos, *, rows, most_h, most_c):
    users, hist = h_own.shape
    cand = c_own.shape[1]
    before = (iota((hist, hist), 0) < iota((hist, hist), 1)).astype(BF)
    for u in range(users):
        parts = []
        for own, row, base, most, pos in (
            (h_own, h_row, 0, most_h, h_pos),
            (c_own, c_row, most_h, most_c, c_pos),
        ):
            n = own.shape[1]
            owner = own[u : u + 1, :]
            match = (iota((rows, n), 0) == owner).astype(F32)
            earlier = dot(match.astype(BF), before[:n, :n], NN)
            rank = jnp.sum(match * earlier, axis=0, keepdims=True).astype(jnp.int32)

            @pl.when(me[0] == u)
            def _():
                pos[...] = owner * 48 + rank

            ids = row[u : u + 1, :]
            high = (match * (ids >> 6).astype(F32)).astype(BF)
            low = (match * (ids & 63).astype(F32)).astype(BF)
            hit = (iota((128, n), 0) == rank + base).astype(BF)
            parts.append(dot(jnp.concatenate([high, low], axis=0), hit, NT))
        both = parts[0] + parts[1]
        req[:, u, :] = (both[:rows] * 64.0 + both[rows:]).astype(jnp.int32)


def gather_kernel(idx, table, out, wide, stage, *, first, count):
    n_rows = table.shape[0]
    chunk = 256

    def widen(i, carry):
        at = pl.multiple_of(i * chunk, chunk)
        block = table[pl.ds(at, chunk), :].astype(F32)
        wide[pl.ds(at, chunk), 0, :] = block[:, :128]
        wide[pl.ds(at, chunk), 1, :] = block[:, 128:]
        return carry

    lax.fori_loop(0, n_rows // chunk, widen, 0)

    def fetch(u, carry):
        for s in range(count):
            stage[s] = wide[idx[u, first + s]]
        out[u] = jnp.concatenate([stage[:, 0, :], stage[:, 1, :]], axis=0).astype(BF)
        return carry

    lax.fori_loop(0, out.shape[0], fetch, 0)


def add_rows(idx, grads, stage, sums, first, count):
    def add(u, carry):
        block = grads[u].astype(F32)
        stage[:, 0, :] = block[:count]
        stage[:, 1, :] = block[count:]
        for s in range(count):
            total = sums[s % len(sums)]
            at = idx[u, first + s]
            total[at] = total[at] + stage[s]
        return carry

    lax.fori_loop(0, grads.shape[0], add, 0)


def scatter_first_kernel(idx, grads, out, stage, other, *, first, count):
    out[...] = jnp.zeros_like(out)
    other[...] = jnp.zeros_like(other)
    add_rows(idx, grads, stage, (out, other), first, count)
    chunk = 128

    def finish(i, carry):
        at = pl.ds(pl.multiple_of(i * chunk, chunk), chunk)
        out[at] = out[at] + other[at]
        return carry

    lax.fori_loop(0, out.shape[0] // chunk, finish, 0)


def scatter_last_kernel(idx, grads, start, out, stage, pair, *, first, count):
    add_rows(idx, grads, stage, (start,), first, count)
    chunk = pair.shape[0]

    def finish(i, carry):
        at = pl.ds(pl.multiple_of(i * chunk, chunk), chunk)
        pair[...] = start[at]
        out[at, 0:128] = pair[:, 0, :]
        out[at, 128:256] = pair[:, 1, :]
        return carry

    lax.fori_loop(0, out.shape[0] // chunk, finish, 0)


def prepare_kernel(recv, h_pos, c_pos, wq, pt_h, pt_c, cand, q1, wq0, sems):
    load = pltpu.make_async_copy(wq.at[0], wq0, sems.at[0])
    load.start()
    slots, hist = pt_h.shape
    n_cand = cand.shape[0]
    cols = recv.shape[1]
    for at in range(0, slots, 256):
        place = iota((256, n_cand), 0) + at
        pt_c[at : at + 256, 0:n_cand] = jnp.where(place == c_pos[...], 1.0, 0.0).astype(BF)
        pt_c[at : at + 256, n_cand:] = jnp.where(place == c_pos[...] + 24, 1.0, 0.0).astype(BF)
    for c in range(0, cols, 2):
        both = jnp.concatenate([recv[:, c].reshape(slots, 128), recv[:, c + 1].reshape(slots, 128)], axis=1)
        got = dot(pt_c[...], both, TN).astype(BF)
        for k in range(2):
            at = (c + k) * 256
            cand[:, at : at + 128] = got[:n_cand, k * 128 : k * 128 + 128]
            cand[:, at + 128 : at + 256] = got[n_cand:, k * 128 : k * 128 + 128]
    load.wait()
    q1[...] = dot(cand[...], wq0[...], NN).astype(BF)
    for at in range(0, slots, 256):
        place = iota((256, hist), 0) + at
        pt_h[at : at + 256, :] = jnp.where(place == h_pos[...], 1.0, 0.0).astype(BF)


def user_kernel(
    length, recv_in, pt_in, cand_in, q1_in, wq_in, wo_in, lg_row, sw, u_row,
    send_out, d_q_out, d_stream_out, logits,
    recv, pt_h, cand, q1, wq1, wo0, keys, q2, att1, soft, d_keys, d_q, d_att, d_stream, in_sems, out_sems,
):
    hist = keys.shape[0]
    n_cand = cand.shape[0]
    cols = recv_in.shape[1]
    rows = recv_in.shape[0]
    slots = pt_h.shape[0]
    inv_root = 1.0 / math.sqrt(128)
    pairs = [(pt_in, pt_h)] + [(recv_in.at[:, c], recv.at[c]) for c in range(cols)]
    pairs += [(q1_in, q1), (cand_in, cand), (wo_in.at[0], wo0), (wq_in.at[1], wq1)]
    loads = [pltpu.make_async_copy(src, dst, in_sems.at[i]) for i, (src, dst) in enumerate(pairs)]
    for load in loads:
        load.start()
    loads[0].wait()
    for c in range(cols):
        loads[1 + c].wait()
        both = jnp.concatenate(
            [recv[c, :, 0:48, :].reshape(slots, 128), recv[c, :, 48:96, :].reshape(slots, 128)], axis=1
        )
        keys[:, c * 256 : c * 256 + 256] = dot(pt_h[...], both, TN).astype(BF)
    for load in loads[1 + cols :]:
        load.wait()

    lg = jnp.transpose(jnp.broadcast_to(lg_row[...], (8, n_cand)))[:, 0:1]
    bias = jnp.where(iota((1, hist), 1) < length[0], 0.0, -1e30)
    scale = inv_root * math.log2(math.e)

    def softmax(q, k):
        scores = dot(q, k, NT) + bias
        top = jnp.max(scores, axis=1, keepdims=True)
        e = jnp.exp2((scores - top) * scale)
        return e * (1.0 / jnp.sum(e, axis=1, keepdims=True))

    def first_layer(h, carry):
        hs = pl.ds(pl.multiple_of(h * 128, 128), 128)
        k = keys[:, hs]
        y = softmax(q1[:, hs], k)
        soft[h] = y
        att1[:, hs] = dot(y.astype(BF), k, NN).astype(BF)
        return carry

    lax.fori_loop(0, HEADS, first_layer, 0)
    stream = cand[...].astype(F32) + dot(att1[...], wo0[...], NN)
    q2[...] = dot(stream.astype(BF), wq1[...], NN).astype(BF)
    score = jnp.sum(stream * sw[...], axis=1, keepdims=True)
    lgs = lg * inv_root

    def second_layer(h, score):
        hs = pl.ds(pl.multiple_of(h * 128, 128), 128)
        k = keys[:, hs]
        q = q2[:, hs]
        u = u_row[:, hs]
        y = softmax(q, k)
        w = y.astype(BF)
        attended = dot(w, k, NN).astype(BF).astype(F32)
        u_hi = u.astype(BF).astype(F32)
        u_mid = (u - u_hi).astype(BF).astype(F32)
        u_low = u - u_hi - u_mid
        line = iota((8, 128), 0)
        pieces = jnp.where(line == 0, u_hi, jnp.where(line == 1, u_mid, jnp.where(line == 2, u_low, 0.0)))
        g = jnp.sum(dot(pieces.astype(BF), k, NT), axis=0, keepdims=True)
        mean = jnp.sum(y * g, axis=1, keepdims=True)
        ds = (y * lgs * (g - mean)).astype(BF)
        d_q[:, hs] = dot(ds, k, NN).astype(BF)
        da = (lg * u).astype(BF)
        d_keys[:, hs] = dot(ds, q, TN) + dot(w, da, TN)
        return score + jnp.sum(attended * u, axis=1, keepdims=True)

    score = lax.fori_loop(0, HEADS, second_layer, score)
    logits[...] = score
    d_after = lg * sw[...] + dot(d_q[...], wq1[...], NT).astype(BF).astype(F32)
    d_stream[...] = d_after
    d_att[...] = dot(d_after.astype(BF), wo0[...], NT).astype(BF)
    put_stream = pltpu.make_async_copy(d_stream, d_stream_out, out_sems.at[0])
    put_stream.start()

    def first_back(h, carry):
        hs = pl.ds(pl.multiple_of(h * 128, 128), 128)
        k = keys[:, hs]
        y = soft[h]
        da = d_att[:, hs]
        dw = dot(da, k, NT)
        mean = jnp.sum(y * dw, axis=1, keepdims=True)
        ds = (y * (dw - mean)).astype(BF)
        d_q[:, hs] = (dot(ds, k, NN) * inv_root).astype(BF)
        grad = d_keys[:, hs] + dot(ds, q1[:, hs], TN) * inv_root + dot(y.astype(BF), da, TN)
        keys[:, hs] = grad.astype(BF)
        return carry

    lax.fori_loop(0, HEADS, first_back, 0)
    puts = [put_stream, pltpu.make_async_copy(d_q, d_q_out, out_sems.at[1])]
    puts[1].start()
    for c in range(cols):
        got = dot(pt_h[...], keys[:, c * 256 : c * 256 + 256], NN).astype(BF)
        recv[c, :, 0:48, :] = got[:, :128].reshape(rows, 48, 128)
        recv[c, :, 48:96, :] = got[:, 128:].reshape(rows, 48, 128)
        put = pltpu.make_async_copy(recv.at[c], send_out.at[:, c], out_sems.at[2 + c])
        put.start()
        puts.append(put)
    for put in puts:
        put.wait()


def finish_kernel(d_q, d_stream, pt_c, wq_in, send, wq0, grad, sem):
    load = pltpu.make_async_copy(wq_in.at[0], wq0, sem.at[0])
    load.start()
    load.wait()
    rows, cols = send.shape[0], send.shape[1]
    grad[...] = (d_stream[...] + dot(d_q[...], wq0[...], NT).astype(BF).astype(F32)).astype(BF)
    for c in range(0, cols, 2):
        at = c * 256
        even = jnp.concatenate([grad[:, at : at + 128], grad[:, at + 256 : at + 384]], axis=1)
        odd = jnp.concatenate([grad[:, at + 128 : at + 256], grad[:, at + 384 : at + 512]], axis=1)
        got = dot(pt_c[...], jnp.concatenate([even, odd], axis=0), NN).astype(BF)
        send[:, c] = got[:, :128].reshape(rows, 48, 128)
        send[:, c + 1] = got[:, 128:].reshape(rows, 48, 128)


def call(kernel, name, mib, out_shape, in_specs, out_specs, scratch=(), **static):
    return pl.pallas_call(
        functools.partial(kernel, **static),
        out_shape=out_shape,
        in_specs=in_specs,
        out_specs=out_specs,
        scratch_shapes=list(scratch),
        compiler_params=pltpu.CompilerParams(vmem_limit_bytes=mib * MIB),
        name=name,
    )


def shape(dims, kind):
    return jax.ShapeDtypeStruct(dims, kind)


def body(
    history_owner, history_row, candidate_owner, candidate_row, history_length,
    embed_table, query_weight, output_weight, score_weight, logit_grad,
):
    n_rows = lax.axis_size("rows")
    n_cols = lax.axis_size("cols")
    users, hist = history_row.shape
    cand = candidate_row.shape[1]
    most_h = 3 * hist // (2 * n_rows)
    most_c = 3 * cand // (2 * n_rows)
    table_rows, col_width = embed_table.shape
    width = n_cols * col_width
    peers = n_rows * n_cols
    slots = n_rows * most_h
    me = lax.axis_index("cols").astype(jnp.int32)
    V, S, A = VMEM_SPEC, SMEM_SPEC, pl.BlockSpec(memory_space=pl.ANY)
    req, h_pos, c_pos = call(
        request_kernel, "requests", 16,
        (shape((n_rows, users, 128), jnp.int32), shape((1, hist), jnp.int32), shape((1, cand), jnp.int32)),
        [S, V, V, V, V], (V, V, V), rows=n_rows, most_h=most_h, most_c=most_c,
    )(me.reshape(1), history_owner[:, :, 0], history_row, candidate_owner[:, :, 0], candidate_row)
    wanted = lax.all_to_all(req, "rows", split_axis=0, concat_axis=0, tiled=True)
    wanted = wanted.reshape(peers, 128)

    def gather(first, count):
        return call(
            gather_kernel, "gather_rows", 16, shape((peers, 2 * count, 128), BF), [S, V], V,
            [pltpu.VMEM((table_rows, 2, 128), F32), pltpu.VMEM((count, 2, 128), F32)],
            first=first, count=count,
        )

    def exchange(x, label):
        with jax.named_scope(label):
            return lax.all_to_all(x, ("rows", "cols"), split_axis=0, concat_axis=0, tiled=True)

    found_c = gather(most_h, most_c)(wanted, embed_table)
    back_c = exchange(found_c, "fetch_c")
    found_h = gather(0, most_h)(wanted, embed_table)
    back_h = exchange(found_h, "fetch_h")
    length = lax.dynamic_slice_in_dim(history_length, me, 1)
    with jax.named_scope("score_row"):
        u_row = jnp.dot(
            output_weight[1].astype(F32), score_weight, precision=lax.Precision.HIGHEST
        ).reshape(1, -1)
    pt_h, pt_c, cand_rows, q1 = call(
        prepare_kernel, "prepare", 24,
        (shape((slots, hist), BF), shape((slots, 2 * cand), BF), shape((cand, width), BF), shape((cand, width), BF)),
        [V, V, V, A], (V, V, V, V),
        [pltpu.VMEM((width, width), BF), pltpu.SemaphoreType.DMA((1,))],
    )(back_c.reshape(n_rows, n_cols, 2 * most_c, 128), h_pos, c_pos, query_weight)
    send_h, d_q, d_stream, logits = call(
        user_kernel, "user_pass", 52,
        (
            shape((n_rows, n_cols, 2 * most_h, 128), BF), shape((cand, width), BF),
            shape((cand, width), F32), shape((cand, 1), F32),
        ),
        [S, A, A, A, A, A, A, V, V, V], (A, A, A, V),
        [
            pltpu.VMEM((n_cols, n_rows, 2 * most_h, 128), BF),
            pltpu.VMEM((slots, hist), BF),
            pltpu.VMEM((cand, width), BF),
            pltpu.VMEM((cand, width), BF),
            pltpu.VMEM((width, width), BF),
            pltpu.VMEM((width, width), BF),
            pltpu.VMEM((hist, width), BF),
            pltpu.VMEM((cand, width), BF),
            pltpu.VMEM((cand, width), BF),
            pltpu.VMEM((HEADS, cand, hist), F32),
            pltpu.VMEM((hist, width), F32),
            pltpu.VMEM((cand, width), BF),
            pltpu.VMEM((cand, width), BF),
            pltpu.VMEM((cand, width), F32),
            pltpu.SemaphoreType.DMA((5 + n_cols,)),
            pltpu.SemaphoreType.DMA((2 + n_cols,)),
        ],
    )(
        length, back_h.reshape(n_rows, n_cols, 2 * most_h, 128), pt_h, cand_rows, q1,
        query_weight, output_weight, logit_grad, score_weight.reshape(1, -1), u_row,
    )
    grads_h = exchange(send_h.reshape(peers, 2 * most_h, 128), "return_h")
    send_c = call(
        finish_kernel, "finish", 20, shape((n_rows, n_cols, 2 * most_c, 128), BF), [V, V, V, A], V,
        [pltpu.VMEM((width, width), BF), pltpu.VMEM((cand, width), BF), pltpu.SemaphoreType.DMA((1,))],
    )(d_q, d_stream, pt_c, query_weight)
    grads_c = exchange(send_c.reshape(peers, 2 * most_c, 128), "return_c")
    half = call(
        scatter_first_kernel, "scatter_history", 18, shape((table_rows, 2, 128), F32), [S, V], V,
        [pltpu.VMEM((most_h, 2, 128), F32), pltpu.VMEM((table_rows, 2, 128), F32)],
        first=0, count=most_h,
    )(wanted, grads_h)
    table_grad = call(
        scatter_last_kernel, "scatter_candidates", 18, shape((table_rows, col_width), F32), [S, V, V], V,
        [pltpu.VMEM((most_c, 2, 128), F32), pltpu.VMEM((128, 2, 128), F32)],
        first=most_h, count=most_c,
    )(wanted, grads_c, half)
    return (logits.reshape(1, cand), table_grad)


def solution(mesh):
    in_specs = (
        P("rows", None, None), P("rows", None), P("rows", None, None), P("rows", None), P("rows"),
        P("rows", "cols"), P(), P(), P(), P(("rows", "cols"), None),
    )
    out_specs = (P(("rows", "cols"), None), P("rows", "cols"))
    return jax.shard_map(body, mesh=mesh, in_specs=in_specs, out_specs=out_specs, check_vma=False)
```

```python
import functools
import math

import jax
import jax.numpy as jnp
from jax import lax
from jax.experimental import pallas as pl
from jax.experimental.pallas import tpu as pltpu
from jax.sharding import PartitionSpec as P

HEADS = 8
BF = jnp.bfloat16
F32 = jnp.float32
NN = (((1,), (0,)), ((), ()))
NT = (((1,), (1,)), ((), ()))
TN = (((0,), (0,)), ((), ()))
VMEM_SPEC = pl.BlockSpec(memory_space=pltpu.VMEM)
SMEM_SPEC = pl.BlockSpec(memory_space=pltpu.SMEM)
MIB = 1024 * 1024


def dot(a, b, dims):
    return lax.dot_general(a, b, dims, preferred_element_type=F32)


def iota(shape, axis):
    return lax.broadcasted_iota(jnp.int32, shape, axis)


def request_kernel(me, h_own, h_row, c_own, c_row, req, h_pos, c_pos, *, rows, most_h, most_c):
    users, hist = h_own.shape
    cand = c_own.shape[1]
    before = (iota((hist, hist), 0) < iota((hist, hist), 1)).astype(BF)
    for u in range(users):
        parts = []
        for own, row, base, most, pos in (
            (h_own, h_row, 0, most_h, h_pos),
            (c_own, c_row, most_h, most_c, c_pos),
        ):
            n = own.shape[1]
            owner = own[u : u + 1, :]
            match = (iota((rows, n), 0) == owner).astype(F32)
            earlier = dot(match.astype(BF), before[:n, :n], NN)
            rank = jnp.sum(match * earlier, axis=0, keepdims=True).astype(jnp.int32)

            @pl.when(me[0] == u)
            def _():
                pos[...] = owner * 48 + rank

            ids = row[u : u + 1, :]
            high = (match * (ids >> 6).astype(F32)).astype(BF)
            low = (match * (ids & 63).astype(F32)).astype(BF)
            hit = (iota((128, n), 0) == rank + base).astype(BF)
            parts.append(dot(jnp.concatenate([high, low], axis=0), hit, NT))
        both = parts[0] + parts[1]
        req[:, u, :] = (both[:rows] * 64.0 + both[rows:]).astype(jnp.int32)


def gather_kernel(idx, table, out, wide, stage, *, most_h):
    n_rows = table.shape[0]
    count = stage.shape[0]
    chunk = 256
    flat = wide.reshape(2 * n_rows, 128)
    lines = stage.reshape(2 * count, 128)

    def widen(i, carry):
        at = pl.multiple_of(i * chunk, chunk)
        block = table[pl.ds(at, chunk), :].astype(F32)
        flat[pl.ds(2 * at, chunk, stride=2), :] = block[:, :128]
        flat[pl.ds(2 * at + 1, chunk, stride=2), :] = block[:, 128:]
        return carry

    lax.fori_loop(0, n_rows // chunk, widen, 0)

    def fetch(u, carry):
        for s in range(count):
            stage[s] = wide[idx[u, s]]
        out[u, 0:most_h, :] = lines[pl.ds(0, most_h, stride=2), :].astype(BF)
        out[u, most_h : 2 * most_h, :] = lines[pl.ds(1, most_h, stride=2), :].astype(BF)
        tail = [lines[pl.ds(2 * most_h + half, count - most_h, stride=2), :] for half in range(2)]
        out[u, 2 * most_h :, :] = jnp.concatenate(tail, axis=0).astype(BF)
        return carry

    lax.fori_loop(0, out.shape[0], fetch, 0)


def scatter_kernel(idx, grads, out, stage, *sums, most_h):
    count = stage.shape[0]
    lines = stage.reshape(2 * count, 128)
    for total in sums:
        total[...] = jnp.zeros_like(total)

    def add(u, carry):
        block = grads[u].astype(F32)
        lines[pl.ds(0, most_h, stride=2), :] = block[:most_h]
        lines[pl.ds(1, most_h, stride=2), :] = block[most_h : 2 * most_h]
        lines[pl.ds(2 * most_h, count - most_h, stride=2), :] = block[2 * most_h : most_h + count]
        lines[pl.ds(2 * most_h + 1, count - most_h, stride=2), :] = block[most_h + count :]
        for s in range(count):
            total = sums[s % len(sums)]
            at = idx[u, s]
            total[at] = total[at] + stage[s]
        return carry

    lax.fori_loop(0, grads.shape[0], add, 0)
    chunk = 128
    flats = [total.reshape(2 * out.shape[0], 128) for total in sums]

    def finish(i, carry):
        at = pl.multiple_of(i * chunk, chunk)
        for half in range(2):
            from_rows = pl.ds(2 * at + half, chunk, stride=2)
            total = flats[0][from_rows, :]
            for flat in flats[1:]:
                total = total + flat[from_rows, :]
            out[pl.ds(at, chunk), half * 128 : half * 128 + 128] = total
        return carry

    lax.fori_loop(0, out.shape[0] // chunk, finish, 0)


def user_kernel(
    length, recv_in, wq_in, wo_in, h_pos, c_pos, lg_row, sw, u_row,
    send_out, logits,
    recv, pt_h, pt_c, cand, q1, wq, wo0, keys, q2, att1, soft, d_keys, d_q, d_att, d_stream, in_sems, out_sems,
):
    hist = keys.shape[0]
    n_cand = cand.shape[0]
    rows, cols = recv_in.shape[0], recv_in.shape[1]
    slots = pt_h.shape[0]
    inv_root = 1.0 / math.sqrt(128)
    blocks = [slice(at, at + 256) for at in range(0, n_cand, 256)]
    whole = [slice(0, n_cand)]
    pairs = [(recv_in.at[:, c], recv.at[c]) for c in range(cols)]
    pairs += [(wq_in, wq), (wo_in.at[0], wo0)]
    loads = [pltpu.make_async_copy(src, dst, in_sems.at[i]) for i, (src, dst) in enumerate(pairs)]
    for load in loads:
        load.start()
    for at in range(0, slots, 256):
        place = iota((256, hist), 0) + at
        pt_h[at : at + 256, :] = jnp.where(place == h_pos[...], 1.0, 0.0).astype(BF)
        place = iota((256, n_cand), 0) + at
        pt_c[at : at + 256, 0:n_cand] = jnp.where(place == c_pos[...], 1.0, 0.0).astype(BF)
        pt_c[at : at + 256, n_cand:] = jnp.where(place == c_pos[...] + 24, 1.0, 0.0).astype(BF)

    def slab(c, part):
        return recv[c, :, part[0] : part[1], :].reshape(slots, 128)

    hist_even, hist_odd, cands = (0, 48), (48, 96), (96, 144)
    for c in range(cols):
        loads[c].wait()
        both = jnp.concatenate([slab(c, hist_even), slab(c, hist_odd)], axis=1)
        keys[:, c * 256 : c * 256 + 256] = dot(pt_h[...], both, TN).astype(BF)
        if c % 2:
            got = dot(pt_c[...], jnp.concatenate([slab(c - 1, cands), slab(c, cands)], axis=1), TN).astype(BF)
            for k in range(2):
                at = (c - 1 + k) * 256
                cand[:, at : at + 128] = got[:n_cand, k * 128 : k * 128 + 128]
                cand[:, at + 128 : at + 256] = got[n_cand:, k * 128 : k * 128 + 128]
    for load in loads[cols:]:
        load.wait()
    q1[...] = dot(cand[...], wq[0], NN).astype(BF)

    lg = jnp.transpose(jnp.broadcast_to(lg_row[...], (8, n_cand)))[:, 0:1]
    bias = jnp.where(iota((1, hist), 1) < length[0], 0.0, -1e30)
    scale = inv_root * math.log2(math.e)

    def softmax(scores):
        scores = scores + bias
        top = jnp.max(scores, axis=1, keepdims=True)
        e = jnp.exp2((scores - top) * scale)
        return e * (1.0 / jnp.sum(e, axis=1, keepdims=True))

    def first_layer(h, carry):
        hs = pl.ds(pl.multiple_of(h * 128, 128), 128)
        k = keys[:, hs]
        scores = [dot(q1[b, hs], k, NT) for b in blocks]
        for b, s in zip(blocks, scores):
            y = softmax(s)
            soft[h, b, :] = y
            att1[b, hs] = dot(y.astype(BF), k, NN).astype(BF)
        return carry

    lax.fori_loop(0, HEADS, first_layer, 0)
    stream = cand[...].astype(F32) + dot(att1[...], wo0[...], NN)
    q2[...] = dot(stream.astype(BF), wq[1], NN).astype(BF)
    score = jnp.sum(stream * sw[...], axis=1, keepdims=True)
    lgs = lg * inv_root

    def second_layer(h, score):
        hs = pl.ds(pl.multiple_of(h * 128, 128), 128)
        k = keys[:, hs]
        u = u_row[:, hs]
        u_hi = u.astype(BF).astype(F32)
        u_mid = (u - u_hi).astype(BF).astype(F32)
        u_low = u - u_hi - u_mid
        line = iota((16, 128), 0)
        pieces = jnp.where(line == 0, u_hi, jnp.where(line == 1, u_mid, jnp.where(line == 2, u_low, 0.0)))
        g = jnp.sum(dot(pieces.astype(BF), k, NT), axis=0, keepdims=True)
        scores = [dot(q2[b, hs], k, NT) for b in whole]
        ws, dss = [], []
        for b, s in zip(whole, scores):
            y = softmax(s)
            w = y.astype(BF)
            mean = jnp.sum(y * g, axis=1, keepdims=True)
            ds = (y * lgs[b] * (g - mean)).astype(BF)
            ws.append(w)
            dss.append(ds)
            d_stream[b, hs] = dot(w, k, NN).astype(BF).astype(F32) * u
            d_q[b, hs] = dot(ds, k, NN).astype(BF)
        ds = jnp.concatenate(dss, axis=0)
        w = jnp.concatenate(ws, axis=0)
        d_keys[:, hs] = dot(ds, q2[:, hs], TN) + dot(w, (lg * u).astype(BF), TN)
        return score

    lax.fori_loop(0, HEADS, second_layer, 0)
    score = score + jnp.sum(d_stream[...], axis=1, keepdims=True)
    logits[...] = jnp.transpose(jnp.broadcast_to(score, (n_cand, 128)))[0:1, :]
    d_after = lg * sw[...] + dot(d_q[...], wq[1], NT).astype(BF).astype(F32)
    d_stream[...] = d_after
    d_att[...] = dot(d_after.astype(BF), wo0[...], NT).astype(BF)

    def first_back(h, carry):
        hs = pl.ds(pl.multiple_of(h * 128, 128), 128)
        k = keys[:, hs]
        slopes = [dot(d_att[b, hs], k, NT) for b in blocks]
        total = d_keys[:, hs]
        for b, dw in zip(blocks, slopes):
            y = soft[h, b, :]
            mean = jnp.sum(y * dw, axis=1, keepdims=True)
            ds = (y * (dw - mean)).astype(BF)
            d_q[b, hs] = (dot(ds, k, NN) * inv_root).astype(BF)
            total = total + dot(ds, q1[b, hs], TN) * inv_root + dot(y.astype(BF), d_att[b, hs], TN)
        keys[:, hs] = total.astype(BF)
        return carry

    lax.fori_loop(0, HEADS, first_back, 0)
    att1[...] = (d_stream[...] + dot(d_q[...], wq[0], NT).astype(BF).astype(F32)).astype(BF)
    puts = []
    for c in range(cols):
        if c % 2 == 0:
            at = c * 256
            even = jnp.concatenate([att1[:, at : at + 128], att1[:, at + 256 : at + 384]], axis=1)
            odd = jnp.concatenate([att1[:, at + 128 : at + 256], att1[:, at + 384 : at + 512]], axis=1)
            got = dot(pt_c[...], jnp.concatenate([even, odd], axis=0), NN).astype(BF)
            recv[c, :, cands[0] : cands[1], :] = got[:, :128].reshape(rows, 48, 128)
            recv[c + 1, :, cands[0] : cands[1], :] = got[:, 128:].reshape(rows, 48, 128)
        got = dot(pt_h[...], keys[:, c * 256 : c * 256 + 256], NN).astype(BF)
        recv[c, :, hist_even[0] : hist_even[1], :] = got[:, :128].reshape(rows, 48, 128)
        recv[c, :, hist_odd[0] : hist_odd[1], :] = got[:, 128:].reshape(rows, 48, 128)
        put = pltpu.make_async_copy(recv.at[c], send_out.at[:, c], out_sems.at[c])
        put.start()
        puts.append(put)
    for put in puts:
        put.wait()


def call(kernel, name, mib, out_shape, in_specs, out_specs, scratch=(), **static):
    return pl.pallas_call(
        functools.partial(kernel, **static),
        out_shape=out_shape,
        in_specs=in_specs,
        out_specs=out_specs,
        scratch_shapes=list(scratch),
        compiler_params=pltpu.CompilerParams(vmem_limit_bytes=mib * MIB),
        name=name,
    )


def shape(dims, kind):
    return jax.ShapeDtypeStruct(dims, kind)


def body(
    history_owner, history_row, candidate_owner, candidate_row, history_length,
    embed_table, query_weight, output_weight, score_weight, logit_grad,
):
    n_rows = lax.axis_size("rows")
    n_cols = lax.axis_size("cols")
    users, hist = history_row.shape
    cand = candidate_row.shape[1]
    most_h = 3 * hist // (2 * n_rows)
    most_c = 3 * cand // (2 * n_rows)
    table_rows, col_width = embed_table.shape
    width = n_cols * col_width
    peers = n_rows * n_cols
    slots = n_rows * most_h
    me = lax.axis_index("cols").astype(jnp.int32)
    V, S, A = VMEM_SPEC, SMEM_SPEC, pl.BlockSpec(memory_space=pl.ANY)
    req, h_pos, c_pos = call(
        request_kernel, "requests", 16,
        (shape((n_rows, users, 128), jnp.int32), shape((1, hist), jnp.int32), shape((1, cand), jnp.int32)),
        [S, V, V, V, V], (V, V, V), rows=n_rows, most_h=most_h, most_c=most_c,
    )(me.reshape(1), history_owner[:, :, 0], history_row, candidate_owner[:, :, 0], candidate_row)
    wanted = lax.all_to_all(req, "rows", split_axis=0, concat_axis=0, tiled=True)
    wanted = wanted.reshape(peers, 128)

    def exchange(x):
        return lax.all_to_all(x, ("rows", "cols"), split_axis=0, concat_axis=0, tiled=True)

    count = most_h + most_c
    found = call(
        gather_kernel, "gather_rows", 24, shape((peers, 2 * count, 128), BF), [S, V], V,
        [pltpu.VMEM((table_rows, 2, 128), F32), pltpu.VMEM((count, 2, 128), F32)], most_h=most_h,
    )(wanted, embed_table)
    back = exchange(found)
    length = lax.dynamic_slice_in_dim(history_length, me, 1)
    u_row = jnp.dot(
        output_weight[1].astype(F32), score_weight, precision=lax.Precision.HIGHEST
    ).reshape(1, -1)
    send, logits = call(
        user_kernel, "user_pass", 60,
        (shape((n_rows, n_cols, 2 * count, 128), BF), shape((1, cand), F32)),
        [S, A, A, A, V, V, V, V, V], (A, V),
        [
            pltpu.VMEM((n_cols, n_rows, 2 * count, 128), BF),
            pltpu.VMEM((slots, hist), BF),
            pltpu.VMEM((slots, 2 * cand), BF),
            pltpu.VMEM((cand, width), BF),
            pltpu.VMEM((cand, width), BF),
            pltpu.VMEM(query_weight.shape, BF),
            pltpu.VMEM((width, width), BF),
            pltpu.VMEM((hist, width), BF),
            pltpu.VMEM((cand, width), BF),
            pltpu.VMEM((cand, width), BF),
            pltpu.VMEM((HEADS, cand, hist), F32),
            pltpu.VMEM((hist, width), F32),
            pltpu.VMEM((cand, width), BF),
            pltpu.VMEM((cand, width), BF),
            pltpu.VMEM((cand, width), F32),
            pltpu.SemaphoreType.DMA((2 + n_cols,)),
            pltpu.SemaphoreType.DMA((n_cols,)),
        ],
    )(
        length, back.reshape(n_rows, n_cols, 2 * count, 128), query_weight, output_weight,
        h_pos, c_pos, logit_grad, score_weight.reshape(1, -1), u_row,
    )
    grads = exchange(send.reshape(peers, 2 * count, 128))
    table_grad = call(
        scatter_kernel, "scatter_rows", 32, shape((table_rows, col_width), F32), [S, V], V,
        [pltpu.VMEM((count, 2, 128), F32)] + [pltpu.VMEM((table_rows, 2, 128), F32)] * 2, most_h=most_h,
    )(wanted, grads)
    return (logits, table_grad)


def solution(mesh):
    in_specs = (
        P("rows", None, None), P("rows", None), P("rows", None, None), P("rows", None), P("rows"),
        P("rows", "cols"), P(), P(), P(), P(("rows", "cols"), None),
    )
    out_specs = (P(("rows", "cols"), None), P("rows", "cols"))
    return jax.shard_map(body, mesh=mesh, in_specs=in_specs, out_specs=out_specs, check_vma=False)
```

```python
import functools
import math

import jax
import jax.numpy as jnp
from jax import lax
from jax.experimental import pallas as pl
from jax.experimental.pallas import tpu as pltpu
from jax.sharding import PartitionSpec as P

HEADS = 8
BF = jnp.bfloat16
F32 = jnp.float32
NN = (((1,), (0,)), ((), ()))
NT = (((1,), (1,)), ((), ()))
TN = (((0,), (0,)), ((), ()))
VMEM_SPEC = pl.BlockSpec(memory_space=pltpu.VMEM)
SMEM_SPEC = pl.BlockSpec(memory_space=pltpu.SMEM)
MIB = 1024 * 1024


def dot(a, b, dims):
    return lax.dot_general(a, b, dims, preferred_element_type=F32)


def iota(shape, axis):
    return lax.broadcasted_iota(jnp.int32, shape, axis)


def request_kernel(me, h_own_in, h_row_in, c_own_in, c_row_in, req, h_pos, c_pos, h_own, h_row, c_own, c_row, sems, *, rows, most_h, most_c):
    pairs = ((h_own_in, h_own), (c_own_in, c_own), (h_row_in, h_row), (c_row_in, c_row))
    loads = [pltpu.make_async_copy(src, dst, sems.at[i]) for i, (src, dst) in enumerate(pairs)]
    for load in loads:
        load.start()
    users, hist = h_row.shape
    before = (iota((hist, hist), 0) < iota((hist, hist), 1)).astype(BF)
    for load in loads:
        load.wait()
    for u in range(users):
        parts = []
        for own, row, base, most, pos in (
            (h_own, h_row, 0, most_h, h_pos),
            (c_own, c_row, most_h, most_c, c_pos),
        ):
            n = row.shape[1]
            owner = own[u]
            match = (iota((rows, n), 0) == owner).astype(F32)
            earlier = dot(match.astype(BF), before[:n, :n], NN)
            rank = jnp.sum(match * earlier, axis=0, keepdims=True).astype(jnp.int32)

            @pl.when(me[0] == u)
            def _():
                pos[...] = owner * 48 + rank

            ids = row[u : u + 1, :]
            high = (match * (ids >> 6).astype(F32)).astype(BF)
            low = (match * (ids & 63).astype(F32)).astype(BF)
            hit = (iota((128, n), 0) == rank + base).astype(BF)
            parts.append(dot(jnp.concatenate([high, low], axis=0), hit, NT))
        both = parts[0] + parts[1]
        req[:, u, :] = (both[:rows] * 64.0 + both[rows:]).astype(jnp.int32)


def gather_kernel(idx, table_in, out, table, wide, stage, send, in_sems, out_sems, *, most_h):
    n_rows = table.shape[0]
    count = stage.shape[0]
    pieces = 4
    chunk = 256
    flat = wide.reshape(2 * n_rows, 128)
    lines = stage.reshape(2 * count, 128)
    part = n_rows // pieces
    loads = []
    for i in range(pieces):
        at = pl.ds(i * part, part)
        loads.append(pltpu.make_async_copy(table_in.at[at], table.at[at], in_sems.at[i]))
        loads[i].start()

    def widen(i, carry):
        at = pl.multiple_of(i * chunk, chunk)
        block = table[pl.ds(at, chunk), :].astype(F32)
        flat[pl.ds(2 * at, chunk, stride=2), :] = block[:, :128]
        flat[pl.ds(2 * at + 1, chunk, stride=2), :] = block[:, 128:]
        return carry

    for i in range(pieces):
        loads[i].wait()
        lax.fori_loop(i * part // chunk, (i + 1) * part // chunk, widen, 0)

    def fetch(u, carry):
        for s in range(count):
            stage[s] = wide[idx[u, s]]
        send[u, 0:most_h, :] = lines[pl.ds(0, most_h, stride=2), :].astype(BF)
        send[u, most_h : 2 * most_h, :] = lines[pl.ds(1, most_h, stride=2), :].astype(BF)
        tail = [lines[pl.ds(2 * most_h + half, count - most_h, stride=2), :] for half in range(2)]
        send[u, 2 * most_h :, :] = jnp.concatenate(tail, axis=0).astype(BF)
        return carry

    part = send.shape[0] // pieces
    puts = []
    for i in range(pieces):
        lax.fori_loop(i * part, (i + 1) * part, fetch, 0)
        at = pl.ds(i * part, part)
        puts.append(pltpu.make_async_copy(send.at[at], out.at[at], out_sems.at[i]))
        puts[i].start()
    for put in puts:
        put.wait()


def scatter_kernel(idx, grads_in, out, grads, result, stage, in_sems, out_sems, *sums, most_h):
    count = stage.shape[0]
    lanes = len(sums)
    pieces = 4
    lines = stage.reshape(2 * count, 128)
    part = grads.shape[0] // pieces
    loads = []
    for i in range(pieces):
        at = pl.ds(i * part, part)
        loads.append(pltpu.make_async_copy(grads_in.at[at], grads.at[at], in_sems.at[i]))
        loads[i].start()
    for total in sums:
        total[...] = jnp.zeros_like(total)

    def add(u, carry):
        block = grads[u].astype(F32)
        lines[pl.ds(0, most_h, stride=2), :] = block[:most_h]
        lines[pl.ds(1, most_h, stride=2), :] = block[most_h : 2 * most_h]
        lines[pl.ds(2 * most_h, count - most_h, stride=2), :] = block[2 * most_h : most_h + count]
        lines[pl.ds(2 * most_h + 1, count - most_h, stride=2), :] = block[most_h + count :]
        for first in range(0, count, lanes):
            places = [idx[u, first + k] for k in range(lanes)]
            values = [sums[k][places[k]] + stage[first + k] for k in range(lanes)]
            for k in range(lanes):
                sums[k][places[k]] = values[k]
        return carry

    for i in range(pieces):
        loads[i].wait()
        lax.fori_loop(i * part, (i + 1) * part, add, 0)
    chunk = 128
    n_rows = result.shape[0]
    flats = [total.reshape(2 * n_rows, 128) for total in sums]

    def finish(i, carry):
        at = pl.multiple_of(i * chunk, chunk)
        for half in range(2):
            from_rows = pl.ds(2 * at + half, chunk, stride=2)
            total = flats[0][from_rows, :]
            for flat in flats[1:]:
                total = total + flat[from_rows, :]
            result[pl.ds(at, chunk), half * 128 : half * 128 + 128] = total
        return carry

    part = n_rows // pieces
    puts = []
    for i in range(pieces):
        lax.fori_loop(i * part // chunk, (i + 1) * part // chunk, finish, 0)
        at = pl.ds(i * part, part)
        puts.append(pltpu.make_async_copy(result.at[at], out.at[at], out_sems.at[i]))
        puts[i].start()
    for put in puts:
        put.wait()


def user_kernel(
    length, recv_in, wq_in, wo_in, h_pos, c_pos, lg_row, sw, u_row,
    send_out, logits,
    recv, pt_h, pt_c, cand, q1, wq, wo0, keys, q2, att1, soft, d_keys, d_q, d_att, d_stream, in_sems, out_sems,
):
    hist = keys.shape[0]
    n_cand = cand.shape[0]
    rows, cols = recv_in.shape[0], recv_in.shape[1]
    slots = pt_h.shape[0]
    inv_root = 1.0 / math.sqrt(128)
    blocks = [slice(at, at + 256) for at in range(0, n_cand, 256)]
    whole = [slice(0, n_cand)]
    pairs = [(recv_in.at[:, c], recv.at[c]) for c in range(cols)]
    pairs += [(wq_in, wq), (wo_in.at[0], wo0)]
    loads = [pltpu.make_async_copy(src, dst, in_sems.at[i]) for i, (src, dst) in enumerate(pairs)]
    for load in loads:
        load.start()
    for at in range(0, slots, 256):
        place = iota((256, hist), 0) + at
        pt_h[at : at + 256, :] = jnp.where(place == h_pos[...], 1.0, 0.0).astype(BF)
        place = iota((256, n_cand), 0) + at
        pt_c[at : at + 256, 0:n_cand] = jnp.where(place == c_pos[...], 1.0, 0.0).astype(BF)
        pt_c[at : at + 256, n_cand:] = jnp.where(place == c_pos[...] + 24, 1.0, 0.0).astype(BF)

    def slab(c, part):
        return recv[c, :, part[0] : part[1], :].reshape(slots, 128)

    hist_even, hist_odd, cands = (0, 48), (48, 96), (96, 144)
    for c in range(cols):
        loads[c].wait()
        both = jnp.concatenate([slab(c, hist_even), slab(c, hist_odd)], axis=1)
        keys[:, c * 256 : c * 256 + 256] = dot(pt_h[...], both, TN).astype(BF)
        if c % 2:
            got = dot(pt_c[...], jnp.concatenate([slab(c - 1, cands), slab(c, cands)], axis=1), TN).astype(BF)
            for k in range(2):
                at = (c - 1 + k) * 256
                cand[:, at : at + 128] = got[:n_cand, k * 128 : k * 128 + 128]
                cand[:, at + 128 : at + 256] = got[n_cand:, k * 128 : k * 128 + 128]
    for load in loads[cols:]:
        load.wait()
    q1[...] = dot(cand[...], wq[0], NN).astype(BF)

    lg = jnp.transpose(jnp.broadcast_to(lg_row[...], (8, n_cand)))[:, 0:1]
    bias = jnp.where(iota((1, hist), 1) < length[0], 0.0, -1e30)
    scale = inv_root * math.log2(math.e)

    def softmax(scores):
        scores = scores + bias
        top = jnp.max(scores, axis=1, keepdims=True)
        e = jnp.exp2((scores - top) * scale)
        return e * (1.0 / jnp.sum(e, axis=1, keepdims=True))

    def first_layer(h, carry):
        hs = pl.ds(pl.multiple_of(h * 128, 128), 128)
        k = keys[:, hs]
        scores = [dot(q1[b, hs], k, NT) for b in blocks]
        for b, s in zip(blocks, scores):
            y = softmax(s)
            soft[h, b, :] = y
            att1[b, hs] = dot(y.astype(BF), k, NN).astype(BF)
        return carry

    lax.fori_loop(0, HEADS, first_layer, 0)
    stream = cand[...].astype(F32) + dot(att1[...], wo0[...], NN)
    q2[...] = dot(stream.astype(BF), wq[1], NN).astype(BF)
    score = jnp.sum(stream * sw[...], axis=1, keepdims=True)
    lgs = lg * inv_root

    def second_layer(h, score):
        hs = pl.ds(pl.multiple_of(h * 128, 128), 128)
        k = keys[:, hs]
        u = u_row[:, hs]
        u_hi = u.astype(BF).astype(F32)
        u_mid = (u - u_hi).astype(BF).astype(F32)
        u_low = u - u_hi - u_mid
        line = iota((16, 128), 0)
        pieces = jnp.where(line == 0, u_hi, jnp.where(line == 1, u_mid, jnp.where(line == 2, u_low, 0.0)))
        g = jnp.sum(dot(pieces.astype(BF), k, NT), axis=0, keepdims=True)
        scores = [dot(q2[b, hs], k, NT) for b in whole]
        ws, dss = [], []
        for b, s in zip(whole, scores):
            y = softmax(s)
            w = y.astype(BF)
            mean = jnp.sum(y * g, axis=1, keepdims=True)
            ds = (y * lgs[b] * (g - mean)).astype(BF)
            ws.append(w)
            dss.append(ds)
            d_stream[b, hs] = dot(w, k, NN).astype(BF).astype(F32) * u
            d_q[b, hs] = dot(ds, k, NN).astype(BF)
        ds = jnp.concatenate(dss, axis=0)
        w = jnp.concatenate(ws, axis=0)
        d_keys[:, hs] = dot(ds, q2[:, hs], TN) + dot(w, (lg * u).astype(BF), TN)
        return score

    lax.fori_loop(0, HEADS, second_layer, 0)
    score = score + jnp.sum(d_stream[...], axis=1, keepdims=True)
    logits[...] = jnp.transpose(jnp.broadcast_to(score, (n_cand, 128)))[0:1, :]
    d_after = lg * sw[...] + dot(d_q[...], wq[1], NT).astype(BF).astype(F32)
    d_stream[...] = d_after
    d_att[...] = dot(d_after.astype(BF), wo0[...], NT).astype(BF)

    def first_back(h, carry):
        hs = pl.ds(pl.multiple_of(h * 128, 128), 128)
        k = keys[:, hs]
        slopes = [dot(d_att[b, hs], k, NT) for b in blocks]
        total = d_keys[:, hs]
        for b, dw in zip(blocks, slopes):
            y = soft[h, b, :]
            mean = jnp.sum(y * dw, axis=1, keepdims=True)
            ds = (y * (dw - mean)).astype(BF)
            d_q[b, hs] = (dot(ds, k, NN) * inv_root).astype(BF)
            total = total + dot(ds, q1[b, hs], TN) * inv_root + dot(y.astype(BF), d_att[b, hs], TN)
        keys[:, hs] = total.astype(BF)
        return carry

    lax.fori_loop(0, HEADS, first_back, 0)
    att1[...] = (d_stream[...] + dot(d_q[...], wq[0], NT).astype(BF).astype(F32)).astype(BF)
    puts = []
    for c in range(cols):
        if c % 2 == 0:
            at = c * 256
            even = jnp.concatenate([att1[:, at : at + 128], att1[:, at + 256 : at + 384]], axis=1)
            odd = jnp.concatenate([att1[:, at + 128 : at + 256], att1[:, at + 384 : at + 512]], axis=1)
            got = dot(pt_c[...], jnp.concatenate([even, odd], axis=0), NN).astype(BF)
            recv[c, :, cands[0] : cands[1], :] = got[:, :128].reshape(rows, 48, 128)
            recv[c + 1, :, cands[0] : cands[1], :] = got[:, 128:].reshape(rows, 48, 128)
        got = dot(pt_h[...], keys[:, c * 256 : c * 256 + 256], NN).astype(BF)
        recv[c, :, hist_even[0] : hist_even[1], :] = got[:, :128].reshape(rows, 48, 128)
        recv[c, :, hist_odd[0] : hist_odd[1], :] = got[:, 128:].reshape(rows, 48, 128)
        put = pltpu.make_async_copy(recv.at[c], send_out.at[:, c], out_sems.at[c])
        put.start()
        puts.append(put)
    for put in puts:
        put.wait()


def call(kernel, name, mib, out_shape, in_specs, out_specs, scratch=(), **static):
    return pl.pallas_call(
        functools.partial(kernel, **static),
        out_shape=out_shape,
        in_specs=in_specs,
        out_specs=out_specs,
        scratch_shapes=list(scratch),
        compiler_params=pltpu.CompilerParams(vmem_limit_bytes=mib * MIB),
        name=name,
    )


def shape(dims, kind):
    return jax.ShapeDtypeStruct(dims, kind)


def body(
    history_owner, history_row, candidate_owner, candidate_row, history_length,
    embed_table, query_weight, output_weight, score_weight, logit_grad,
):
    n_rows = lax.axis_size("rows")
    n_cols = lax.axis_size("cols")
    users, hist = history_row.shape
    cand = candidate_row.shape[1]
    most_h = 3 * hist // (2 * n_rows)
    most_c = 3 * cand // (2 * n_rows)
    table_rows, col_width = embed_table.shape
    width = n_cols * col_width
    peers = n_rows * n_cols
    slots = n_rows * most_h
    me = lax.axis_index("cols").astype(jnp.int32)
    V, S, A = VMEM_SPEC, SMEM_SPEC, pl.BlockSpec(memory_space=pl.ANY)
    req, h_pos, c_pos = call(
        request_kernel, "requests", 62,
        (shape((n_rows, users, 128), jnp.int32), shape((1, hist), jnp.int32), shape((1, cand), jnp.int32)),
        [S, A, A, A, A], (V, V, V),
        [
            pltpu.VMEM((users, 1, hist), jnp.int32), pltpu.VMEM((users, hist), jnp.int32),
            pltpu.VMEM((users, 1, cand), jnp.int32), pltpu.VMEM((users, cand), jnp.int32),
            pltpu.SemaphoreType.DMA((4,)),
        ],
        rows=n_rows, most_h=most_h, most_c=most_c,
    )(
        me.reshape(1), history_owner.transpose(0, 2, 1), history_row,
        candidate_owner.transpose(0, 2, 1), candidate_row,
    )
    wanted = lax.all_to_all(req, "rows", split_axis=0, concat_axis=0, tiled=True)
    wanted = wanted.reshape(peers, 128)

    def exchange(x):
        return lax.all_to_all(x, ("rows", "cols"), split_axis=0, concat_axis=0, tiled=True)

    count = most_h + most_c
    found = call(
        gather_kernel, "gather_rows", 62, shape((peers, 2 * count, 128), BF), [S, A], A,
        [
            pltpu.VMEM((table_rows, col_width), BF), pltpu.VMEM((table_rows, 2, 128), F32),
            pltpu.VMEM((count, 2, 128), F32), pltpu.VMEM((peers, 2 * count, 128), BF),
            pltpu.SemaphoreType.DMA((4,)), pltpu.SemaphoreType.DMA((4,)),
        ],
        most_h=most_h,
    )(wanted, embed_table)
    back = exchange(found)
    length = lax.dynamic_slice_in_dim(history_length, me, 1)
    u_row = jnp.dot(
        output_weight[1].astype(F32), score_weight, precision=lax.Precision.HIGHEST
    ).reshape(1, -1)
    send, logits = call(
        user_kernel, "user_pass", 60,
        (shape((n_rows, n_cols, 2 * count, 128), BF), shape((1, cand), F32)),
        [S, A, A, A, V, V, V, V, V], (A, V),
        [
            pltpu.VMEM((n_cols, n_rows, 2 * count, 128), BF),
            pltpu.VMEM((slots, hist), BF),
            pltpu.VMEM((slots, 2 * cand), BF),
            pltpu.VMEM((cand, width), BF),
            pltpu.VMEM((cand, width), BF),
            pltpu.VMEM(query_weight.shape, BF),
            pltpu.VMEM((width, width), BF),
            pltpu.VMEM((hist, width), BF),
            pltpu.VMEM((cand, width), BF),
            pltpu.VMEM((cand, width), BF),
            pltpu.VMEM((HEADS, cand, hist), F32),
            pltpu.VMEM((hist, width), F32),
            pltpu.VMEM((cand, width), BF),
            pltpu.VMEM((cand, width), BF),
            pltpu.VMEM((cand, width), F32),
            pltpu.SemaphoreType.DMA((2 + n_cols,)),
            pltpu.SemaphoreType.DMA((n_cols,)),
        ],
    )(
        length, back.reshape(n_rows, n_cols, 2 * count, 128), query_weight, output_weight,
        h_pos, c_pos, logit_grad, score_weight.reshape(1, -1), u_row,
    )
    grads = exchange(send.reshape(peers, 2 * count, 128))
    table_grad = call(
        scatter_kernel, "scatter_rows", 62, shape((table_rows, col_width), F32), [S, A], A,
        [
            pltpu.VMEM((peers, 2 * count, 128), BF), pltpu.VMEM((table_rows, col_width), F32),
            pltpu.VMEM((count, 2, 128), F32),
            pltpu.SemaphoreType.DMA((4,)), pltpu.SemaphoreType.DMA((4,)),
        ]
        + [pltpu.VMEM((table_rows, 2, 128), F32)] * 4,
        most_h=most_h,
    )(wanted, grads)
    return (logits, table_grad)


def solution(mesh):
    in_specs = (
        P("rows", None, None), P("rows", None), P("rows", None, None), P("rows", None), P("rows"),
        P("rows", "cols"), P(), P(), P(), P(("rows", "cols"), None),
    )
    out_specs = (P(("rows", "cols"), None), P("rows", "cols"))
    return jax.shard_map(body, mesh=mesh, in_specs=in_specs, out_specs=out_specs, check_vma=False)
```

```python
import functools
import math

import jax
import jax.numpy as jnp
from jax import lax
from jax.experimental import pallas as pl
from jax.experimental.pallas import tpu as pltpu
from jax.sharding import PartitionSpec as P

HEADS = 8
BF = jnp.bfloat16
F32 = jnp.float32
NN = (((1,), (0,)), ((), ()))
NT = (((1,), (1,)), ((), ()))
TN = (((0,), (0,)), ((), ()))
VMEM_SPEC = pl.BlockSpec(memory_space=pltpu.VMEM)
SMEM_SPEC = pl.BlockSpec(memory_space=pltpu.SMEM)
MIB = 1024 * 1024


def dot(a, b, dims):
    return lax.dot_general(a, b, dims, preferred_element_type=F32)


def iota(shape, axis):
    return lax.broadcasted_iota(jnp.int32, shape, axis)


def request_kernel(me, h_own_in, h_row_in, c_own_in, c_row_in, req, h_pos, c_pos, h_own, h_row, c_own, c_row, sems, *, rows, most_h, most_c):
    pairs = ((h_own_in, h_own), (c_own_in, c_own), (h_row_in, h_row), (c_row_in, c_row))
    loads = [pltpu.make_async_copy(src, dst, sems.at[i]) for i, (src, dst) in enumerate(pairs)]
    for load in loads:
        load.start()
    users, hist = h_row.shape
    before = (iota((hist, hist), 0) < iota((hist, hist), 1)).astype(BF)
    for load in loads:
        load.wait()
    earlier = []
    for own in (h_own, c_own):
        n = own.shape[2]
        match = jnp.concatenate([(iota((rows, n), 0) == own[u]).astype(F32) for u in range(users)], axis=0)
        earlier.append((match, dot(match.astype(BF), before[:n, :n], NN)))
    for u in range(users):
        parts = []
        for (matches, counts), row, base, pos in (
            (earlier[0], h_row, 0, h_pos),
            (earlier[1], c_row, most_h, c_pos),
        ):
            n = row.shape[1]
            owner = (h_own if pos is h_pos else c_own)[u]
            match = matches[u * rows : (u + 1) * rows]
            rank = jnp.sum(match * counts[u * rows : (u + 1) * rows], axis=0, keepdims=True).astype(jnp.int32)

            @pl.when(me[0] == u)
            def _():
                pos[...] = owner * 48 + rank

            ids = row[u : u + 1, :]
            high = (match * (ids >> 6).astype(F32)).astype(BF)
            low = (match * (ids & 63).astype(F32)).astype(BF)
            hit = (iota((128, n), 0) == rank + base).astype(BF)
            parts.append(dot(jnp.concatenate([high, low], axis=0), hit, NT))
        both = parts[0] + parts[1]
        req[:, u, :] = (both[:rows] * 64.0 + both[rows:]).astype(jnp.int32)


def gather_kernel(idx, table_in, out, table, wide, stage, send, in_sems, out_sems, *, most_h):
    n_rows = table.shape[0]
    count = stage.shape[0]
    pieces = 4
    chunk = 256
    flat = wide.reshape(2 * n_rows, 128)
    lines = stage.reshape(2 * count, 128)
    part = n_rows // pieces
    loads = []
    for i in range(pieces):
        at = pl.ds(i * part, part)
        loads.append(pltpu.make_async_copy(table_in.at[at], table.at[at], in_sems.at[i]))
        loads[i].start()

    def widen(i, carry):
        at = pl.multiple_of(i * chunk, chunk)
        block = table[pl.ds(at, chunk), :].astype(F32)
        flat[pl.ds(2 * at, chunk, stride=2), :] = block[:, :128]
        flat[pl.ds(2 * at + 1, chunk, stride=2), :] = block[:, 128:]
        return carry

    for i in range(pieces):
        loads[i].wait()
        lax.fori_loop(i * part // chunk, (i + 1) * part // chunk, widen, 0)

    def fetch(u, carry):
        for s in range(count):
            stage[s] = wide[idx[u, s]]
        send[u, 0:most_h, :] = lines[pl.ds(0, most_h, stride=2), :].astype(BF)
        send[u, most_h : 2 * most_h, :] = lines[pl.ds(1, most_h, stride=2), :].astype(BF)
        tail = [lines[pl.ds(2 * most_h + half, count - most_h, stride=2), :] for half in range(2)]
        send[u, 2 * most_h :, :] = jnp.concatenate(tail, axis=0).astype(BF)
        return carry

    part = send.shape[0] // pieces
    puts = []
    for i in range(pieces):
        lax.fori_loop(i * part, (i + 1) * part, fetch, 0)
        at = pl.ds(i * part, part)
        puts.append(pltpu.make_async_copy(send.at[at], out.at[at], out_sems.at[i]))
        puts[i].start()
    for put in puts:
        put.wait()


def scatter_kernel(idx, grads_in, out, grads, result, stage, in_sems, out_sems, *sums, most_h):
    count = stage.shape[0]
    lanes = len(sums)
    pieces = 4
    lines = stage.reshape(2 * count, 128)
    part = grads.shape[0] // pieces
    loads = []
    for i in range(pieces):
        at = pl.ds(i * part, part)
        loads.append(pltpu.make_async_copy(grads_in.at[at], grads.at[at], in_sems.at[i]))
        loads[i].start()
    for total in sums:
        total[...] = jnp.zeros_like(total)

    def add(u, carry):
        block = grads[u].astype(F32)
        lines[pl.ds(0, most_h, stride=2), :] = block[:most_h]
        lines[pl.ds(1, most_h, stride=2), :] = block[most_h : 2 * most_h]
        lines[pl.ds(2 * most_h, count - most_h, stride=2), :] = block[2 * most_h : most_h + count]
        lines[pl.ds(2 * most_h + 1, count - most_h, stride=2), :] = block[most_h + count :]
        for first in range(0, count, lanes):
            places = [idx[u, first + k] for k in range(lanes)]
            values = [sums[k][places[k]] + stage[first + k] for k in range(lanes)]
            for k in range(lanes):
                sums[k][places[k]] = values[k]
        return carry

    for i in range(pieces):
        loads[i].wait()
        lax.fori_loop(i * part, (i + 1) * part, add, 0)
    chunk = 128
    n_rows = result.shape[0]
    flats = [total.reshape(2 * n_rows, 128) for total in sums]

    def finish(i, carry):
        at = pl.multiple_of(i * chunk, chunk)
        for half in range(2):
            from_rows = pl.ds(2 * at + half, chunk, stride=2)
            total = flats[0][from_rows, :]
            for flat in flats[1:]:
                total = total + flat[from_rows, :]
            result[pl.ds(at, chunk), half * 128 : half * 128 + 128] = total
        return carry

    part = n_rows // pieces
    puts = []
    for i in range(pieces):
        lax.fori_loop(i * part // chunk, (i + 1) * part // chunk, finish, 0)
        at = pl.ds(i * part, part)
        puts.append(pltpu.make_async_copy(result.at[at], out.at[at], out_sems.at[i]))
        puts[i].start()
    for put in puts:
        put.wait()


def user_kernel(
    length, recv_in, wq_in, wo_in, h_pos, c_pos, lg_row, sw, u_row,
    send_out, logits,
    recv, pt_h, pt_c, cand, q1, wq, wo0, keys, q2, att1, soft, d_keys, d_q, d_att, d_stream, in_sems, out_sems,
):
    hist = keys.shape[0]
    n_cand = cand.shape[0]
    rows, cols = recv_in.shape[0], recv_in.shape[1]
    slots = pt_h.shape[0]
    inv_root = 1.0 / math.sqrt(128)
    blocks = [slice(at, at + 256) for at in range(0, n_cand, 256)]
    whole = [slice(0, n_cand)]
    pairs = [(recv_in.at[:, c], recv.at[c]) for c in range(cols)]
    pairs += [(wq_in, wq), (wo_in.at[0], wo0)]
    loads = [pltpu.make_async_copy(src, dst, in_sems.at[i]) for i, (src, dst) in enumerate(pairs)]
    for load in loads:
        load.start()
    for at in range(0, slots, 256):
        place = iota((256, hist), 0) + at
        pt_h[at : at + 256, :] = jnp.where(place == h_pos[...], 1.0, 0.0).astype(BF)
        place = iota((256, n_cand), 0) + at
        pt_c[at : at + 256, 0:n_cand] = jnp.where(place == c_pos[...], 1.0, 0.0).astype(BF)
        pt_c[at : at + 256, n_cand:] = jnp.where(place == c_pos[...] + 24, 1.0, 0.0).astype(BF)

    def slab(c, part):
        return recv[c, :, part[0] : part[1], :].reshape(slots, 128)

    hist_even, hist_odd, cands = (0, 48), (48, 96), (96, 144)
    for load in loads[:cols]:
        load.wait()
    got = dot(pt_c[...], jnp.concatenate([slab(c, cands) for c in range(cols)], axis=1), TN).astype(BF)
    for c in range(cols):
        at = c * 256
        cand[:, at : at + 128] = got[:n_cand, c * 128 : c * 128 + 128]
        cand[:, at + 128 : at + 256] = got[n_cand:, c * 128 : c * 128 + 128]
    for c in range(0, cols, 2):
        slabs = [slab(c + k, part) for k in range(2) for part in (hist_even, hist_odd)]
        keys[:, c * 256 : c * 256 + 512] = dot(pt_h[...], jnp.concatenate(slabs, axis=1), TN).astype(BF)
    for load in loads[cols:]:
        load.wait()
    q1[...] = dot(cand[...], wq[0], NN).astype(BF)

    lg = jnp.transpose(jnp.broadcast_to(lg_row[...], (8, n_cand)))[:, 0:1]
    bias = jnp.where(iota((1, hist), 1) < length[0], 0.0, -1e30)
    scale = inv_root * math.log2(math.e)

    def softmax(scores):
        scores = scores + bias
        top = jnp.max(scores, axis=1, keepdims=True)
        e = jnp.exp2((scores - top) * scale)
        return e * (1.0 / jnp.sum(e, axis=1, keepdims=True))

    def first_layer(h, carry):
        hs = pl.ds(pl.multiple_of(h * 128, 128), 128)
        k = keys[:, hs]
        scores = [dot(q1[b, hs], k, NT) for b in blocks]
        for b, s in zip(blocks, scores):
            y = softmax(s)
            soft[h, b, :] = y
            att1[b, hs] = dot(y.astype(BF), k, NN).astype(BF)
        return carry

    lax.fori_loop(0, HEADS, first_layer, 0)
    stream = cand[...].astype(F32) + dot(att1[...], wo0[...], NN)
    q2[...] = dot(stream.astype(BF), wq[1], NN).astype(BF)
    score = jnp.sum(stream * sw[...], axis=1, keepdims=True)
    lgs = lg * inv_root

    def second_layer(h, score):
        hs = pl.ds(pl.multiple_of(h * 128, 128), 128)
        k = keys[:, hs]
        u = u_row[:, hs]
        u_hi = u.astype(BF).astype(F32)
        u_mid = (u - u_hi).astype(BF).astype(F32)
        u_low = u - u_hi - u_mid
        line = iota((16, 128), 0)
        pieces = jnp.where(line == 0, u_hi, jnp.where(line == 1, u_mid, jnp.where(line == 2, u_low, 0.0)))
        g = jnp.sum(dot(pieces.astype(BF), k, NT), axis=0, keepdims=True)
        scores = [dot(q2[b, hs], k, NT) for b in whole]
        ws, dss = [], []
        for b, s in zip(whole, scores):
            y = softmax(s)
            w = y.astype(BF)
            mean = jnp.sum(y * g, axis=1, keepdims=True)
            ds = (y * lgs[b] * (g - mean)).astype(BF)
            ws.append(w)
            dss.append(ds)
            d_stream[b, hs] = dot(w, k, NN).astype(BF).astype(F32) * u
            d_q[b, hs] = dot(ds, k, NN).astype(BF)
        ds = jnp.concatenate(dss, axis=0)
        w = jnp.concatenate(ws, axis=0)
        d_keys[:, hs] = dot(ds, q2[:, hs], TN) + dot(w, (lg * u).astype(BF), TN)
        return score

    lax.fori_loop(0, HEADS, second_layer, 0)
    score = score + jnp.sum(d_stream[...], axis=1, keepdims=True)
    logits[...] = jnp.transpose(jnp.broadcast_to(score, (n_cand, 128)))[0:1, :]
    d_after = lg * sw[...] + dot(d_q[...], wq[1], NT).astype(BF).astype(F32)
    d_stream[...] = d_after
    d_att[...] = dot(d_after.astype(BF), wo0[...], NT).astype(BF)

    def first_back(h, carry):
        hs = pl.ds(pl.multiple_of(h * 128, 128), 128)
        k = keys[:, hs]
        slopes = [dot(d_att[b, hs], k, NT) for b in blocks]
        total = d_keys[:, hs]
        for b, dw in zip(blocks, slopes):
            y = soft[h, b, :]
            mean = jnp.sum(y * dw, axis=1, keepdims=True)
            ds = (y * (dw - mean)).astype(BF)
            d_q[b, hs] = (dot(ds, k, NN) * inv_root).astype(BF)
            total = total + dot(ds, q1[b, hs], TN) * inv_root + dot(y.astype(BF), d_att[b, hs], TN)
        keys[:, hs] = total.astype(BF)
        return carry

    lax.fori_loop(0, HEADS, first_back, 0)
    att1[...] = (d_stream[...] + dot(d_q[...], wq[0], NT).astype(BF).astype(F32)).astype(BF)
    puts = []
    for c in range(cols):
        if c % 2 == 0:
            at = c * 256
            even = jnp.concatenate([att1[:, at : at + 128], att1[:, at + 256 : at + 384]], axis=1)
            odd = jnp.concatenate([att1[:, at + 128 : at + 256], att1[:, at + 384 : at + 512]], axis=1)
            got = dot(pt_c[...], jnp.concatenate([even, odd], axis=0), NN).astype(BF)
            recv[c, :, cands[0] : cands[1], :] = got[:, :128].reshape(rows, 48, 128)
            recv[c + 1, :, cands[0] : cands[1], :] = got[:, 128:].reshape(rows, 48, 128)
        got = dot(pt_h[...], keys[:, c * 256 : c * 256 + 256], NN).astype(BF)
        recv[c, :, hist_even[0] : hist_even[1], :] = got[:, :128].reshape(rows, 48, 128)
        recv[c, :, hist_odd[0] : hist_odd[1], :] = got[:, 128:].reshape(rows, 48, 128)
        put = pltpu.make_async_copy(recv.at[c], send_out.at[:, c], out_sems.at[c])
        put.start()
        puts.append(put)
    for put in puts:
        put.wait()


def call(kernel, name, mib, out_shape, in_specs, out_specs, scratch=(), **static):
    return pl.pallas_call(
        functools.partial(kernel, **static),
        out_shape=out_shape,
        in_specs=in_specs,
        out_specs=out_specs,
        scratch_shapes=list(scratch),
        compiler_params=pltpu.CompilerParams(vmem_limit_bytes=mib * MIB),
        name=name,
    )


def shape(dims, kind):
    return jax.ShapeDtypeStruct(dims, kind)


def body(
    history_owner, history_row, candidate_owner, candidate_row, history_length,
    embed_table, query_weight, output_weight, score_weight, logit_grad,
):
    n_rows = lax.axis_size("rows")
    n_cols = lax.axis_size("cols")
    users, hist = history_row.shape
    cand = candidate_row.shape[1]
    most_h = 3 * hist // (2 * n_rows)
    most_c = 3 * cand // (2 * n_rows)
    table_rows, col_width = embed_table.shape
    width = n_cols * col_width
    peers = n_rows * n_cols
    slots = n_rows * most_h
    me = lax.axis_index("cols").astype(jnp.int32)
    V, S, A = VMEM_SPEC, SMEM_SPEC, pl.BlockSpec(memory_space=pl.ANY)
    req, h_pos, c_pos = call(
        request_kernel, "requests", 62,
        (shape((n_rows, users, 128), jnp.int32), shape((1, hist), jnp.int32), shape((1, cand), jnp.int32)),
        [S, A, A, A, A], (V, V, V),
        [
            pltpu.VMEM((users, 1, hist), jnp.int32), pltpu.VMEM((users, hist), jnp.int32),
            pltpu.VMEM((users, 1, cand), jnp.int32), pltpu.VMEM((users, cand), jnp.int32),
            pltpu.SemaphoreType.DMA((4,)),
        ],
        rows=n_rows, most_h=most_h, most_c=most_c,
    )(
        me.reshape(1), history_owner.transpose(0, 2, 1), history_row,
        candidate_owner.transpose(0, 2, 1), candidate_row,
    )
    wanted = lax.all_to_all(req, "rows", split_axis=0, concat_axis=0, tiled=True)
    wanted = wanted.reshape(peers, 128)

    def exchange(x):
        return lax.all_to_all(x, ("rows", "cols"), split_axis=0, concat_axis=0, tiled=True)

    count = most_h + most_c
    found = call(
        gather_kernel, "gather_rows", 62, shape((peers, 2 * count, 128), BF), [S, A], A,
        [
            pltpu.VMEM((table_rows, col_width), BF), pltpu.VMEM((table_rows, 2, 128), F32),
            pltpu.VMEM((count, 2, 128), F32), pltpu.VMEM((peers, 2 * count, 128), BF),
            pltpu.SemaphoreType.DMA((4,)), pltpu.SemaphoreType.DMA((4,)),
        ],
        most_h=most_h,
    )(wanted, embed_table)
    back = exchange(found)
    length = lax.dynamic_slice_in_dim(history_length, me, 1)
    u_row = jnp.dot(
        output_weight[1].astype(F32), score_weight, precision=lax.Precision.HIGHEST
    ).reshape(1, -1)
    send, logits = call(
        user_kernel, "user_pass", 60,
        (shape((n_rows, n_cols, 2 * count, 128), BF), shape((1, cand), F32)),
        [S, A, A, A, V, V, V, V, V], (A, V),
        [
            pltpu.VMEM((n_cols, n_rows, 2 * count, 128), BF),
            pltpu.VMEM((slots, hist), BF),
            pltpu.VMEM((slots, 2 * cand), BF),
            pltpu.VMEM((cand, width), BF),
            pltpu.VMEM((cand, width), BF),
            pltpu.VMEM(query_weight.shape, BF),
            pltpu.VMEM((width, width), BF),
            pltpu.VMEM((hist, width), BF),
            pltpu.VMEM((cand, width), BF),
            pltpu.VMEM((cand, width), BF),
            pltpu.VMEM((HEADS, cand, hist), F32),
            pltpu.VMEM((hist, width), F32),
            pltpu.VMEM((cand, width), BF),
            pltpu.VMEM((cand, width), BF),
            pltpu.VMEM((cand, width), F32),
            pltpu.SemaphoreType.DMA((2 + n_cols,)),
            pltpu.SemaphoreType.DMA((n_cols,)),
        ],
    )(
        length, back.reshape(n_rows, n_cols, 2 * count, 128), query_weight, output_weight,
        h_pos, c_pos, logit_grad, score_weight.reshape(1, -1), u_row,
    )
    grads = exchange(send.reshape(peers, 2 * count, 128))
    table_grad = call(
        scatter_kernel, "scatter_rows", 62, shape((table_rows, col_width), F32), [S, A], A,
        [
            pltpu.VMEM((peers, 2 * count, 128), BF), pltpu.VMEM((table_rows, col_width), F32),
            pltpu.VMEM((count, 2, 128), F32),
            pltpu.SemaphoreType.DMA((4,)), pltpu.SemaphoreType.DMA((4,)),
        ]
        + [pltpu.VMEM((table_rows, 2, 128), F32)] * 4,
        most_h=most_h,
    )(wanted, grads)
    return (logits, table_grad)


def solution(mesh):
    in_specs = (
        P("rows", None, None), P("rows", None), P("rows", None, None), P("rows", None), P("rows"),
        P("rows", "cols"), P(), P(), P(), P(("rows", "cols"), None),
    )
    out_specs = (P(("rows", "cols"), None), P("rows", "cols"))
    return jax.shard_map(body, mesh=mesh, in_specs=in_specs, out_specs=out_specs, check_vma=False)
```
